32 devices in a mesh: leaf: 8 (over z, x), task: 4 (over y, core).
Axes of the slice: x: 2, y: 2, z: 4, core: 2. Of those that a mesh axis runs over, the one named last changes fastest.
Arguments:
- points: bfloat16 [131072, 64], P(('leaf', 'task')), may hold values from -6 to 6
- weights: bfloat16 [131072, 64], P(('leaf', 'task')), may hold values from -4 to 4
- point_order: int32 [8, 4, 4096], P('leaf', 'task'), may hold values from 0 to 4095, each once within a row
- node_order: int32 [8, 4, 4096], P('leaf', 'task'), may hold values from 0 to 4095, each once within a row
- merge_order: int32 [8, 4, 2, 1024], P('leaf', 'task'), may hold values from 0 to 1023, as said below
- far_list: int32 [8, 4, 4, 3], P('leaf', 'task'), may hold values 0 or 1
- task_target: int32 [8, 4, 4, 1], P('leaf', 'task'), may hold values from -1 to 3, as said below
- task_source: int32 [8, 4, 4, 1], P('leaf', 'task'), may hold values from 0 to 3
Outputs:
- potentials: float32 [131072, 64], P(('leaf', 'task'))
The draws below stay inside these ranges and needn't reach their ends.
Inputs may be any that keep to these rules, and one draw needn't show every extreme that they name: `merge_order`: each row is a permutation of 0 to 1023; rows [i, j, b] are equal for all i with the same i // 2 ** (b + 1). `task_target`: -1 marks an empty slot; every device of every draw has a slab toward which all 1 slots are used.
All inputs are finite; a program needn't handle non-finite values. No bound on the sum of `far_list` on one device may be relied on, other than what follows from the above.
Results may differ from the reference program's by a relative error of at most 0.002.
Values may be sent and summed in bfloat16 or wider, within the bound.
A program may use at most 64 MiB of HBM per device.

```python
import jax
import jax.numpy as jnp
from jax import lax

F = 64
C = 64
LEAF_PTS = 1024
SKEL = 512
LEVELS = 3
LEAF_DEV = 4
CAP = 1
PTS_DEV = 4096
MERGES = 2
REGIONS = 8
SLABS = 4
POINTS = 131072


def draw_merge_order(key, part):
    base_key = jax.random.fold_in(key, 7)
    key_list = jax.random.split(base_key, REGIONS * SLABS * MERGES)
    shuffles = jax.vmap(lambda one_key: jax.random.permutation(one_key, 2 * SKEL))(key_list)
    shuffles = shuffles.reshape(REGIONS, SLABS, MERGES, 2 * SKEL)
    per_tier = []
    for tier_index in range(MERGES):
        stride_len = 2 ** (tier_index + 1)
        leaders = jnp.arange(REGIONS) // stride_len * stride_len
        per_tier.append(shuffles[leaders, :, tier_index, :])
    return jnp.stack(per_tier, axis=2).astype(jnp.int32)


def draw_task_target(key, part):
    busy_key, roll_key, leaf_key = jax.random.split(jax.random.fold_in(key, 11), 3)
    busyness = jax.random.randint(busy_key, (REGIONS, 1, SLABS, 1), 1, 5)
    rolled = jax.random.randint(roll_key, (REGIONS, SLABS, SLABS, CAP), 0, 4)
    chosen = jax.random.randint(leaf_key, (REGIONS, SLABS, SLABS, CAP), 0, LEAF_DEV)
    sender = jnp.arange(SLABS)[None, :, None, None]
    receiver = jnp.arange(SLABS)[None, None, :, None]
    forced = receiver == (sender + 1) % SLABS
    return jnp.where((rolled < busyness) | forced, chosen, -1).astype(jnp.int32)


def with_ends(array, rng, smallest, top_value):
    index_at = [jax.random.randint(jax.random.fold_in(rng, axis), (), 0, length) for axis, length in enumerate(array.shape)]
    main_axis = array.shape.index(max(array.shape))
    neighbour = index_at[:main_axis] + [(index_at[main_axis] + 1) % array.shape[main_axis]] + index_at[main_axis + 1:]
    return array.at[tuple(index_at)].set(smallest).at[tuple(neighbour)].set(top_value)


def steps_of(own_key, shape, cuts, low, top_value):
    def one(position, parts):
        draws = jax.random.uniform(jax.random.fold_in(jax.random.fold_in(own_key, 6), position), (parts,), jnp.float32, low / len(cuts), top_value / len(cuts))
        return jnp.repeat(jnp.exp(draws), shape[position] // parts).reshape((-1,) + (1,) * (len(shape) - position - 1))

    factor_of = one(*cuts[0])
    for cut in cuts[1:]:
        factor_of = factor_of * one(*cut)
    return factor_of


def noise(stream_key, extent, width, most, cuts=(), held_as=jnp.bfloat16):
    values = jax.random.normal(stream_key, extent, jnp.float32) * width
    if len(cuts) > 0:
        values = steps_of(stream_key, extent, cuts, -0.22, 0.18) * values
    return jnp.clip(values, min=-most, max=most).astype(held_as)


def setup_inputs(seed: int = 0) -> dict:
    key_of = jax.random.split(jax.random.key(seed), 9)
    return {
        "points": noise(key_of[0], (POINTS, F), 1.0, 6.0, ((0, 32),)),
        "weights": noise(key_of[1], (POINTS, C), 0.5, 4.0, ((0, 32),)),
        "point_order": jax.vmap(lambda own: jax.random.permutation(own, PTS_DEV))(jax.random.split(key_of[2], REGIONS * SLABS)).reshape((REGIONS, SLABS, PTS_DEV)).astype(jnp.int32),
        "node_order": jax.vmap(lambda own: jax.random.permutation(own, PTS_DEV))(jax.random.split(key_of[3], REGIONS * SLABS)).reshape((REGIONS, SLABS, PTS_DEV)).astype(jnp.int32),
        "merge_order": draw_merge_order(jax.random.fold_in(key_of[8], 71), 0),
        "far_list": with_ends((jax.random.randint(key_of[5], (REGIONS, SLABS, LEAF_DEV, LEVELS), 0, 4) < 3).astype(jnp.int32), jax.random.fold_in(key_of[5], 1), 0, 1),
        "task_target": draw_task_target(jax.random.fold_in(key_of[8], 71), 0),
        "task_source": with_ends(jax.random.randint(key_of[7], (REGIONS, SLABS, SLABS, CAP), 0, LEAF_DEV), jax.random.fold_in(key_of[7], 1), 0, LEAF_DEV - 1).astype(jnp.int32),
    }


KERNEL_SCALE = 1.5


def kernel(left_pts, right_pts):
    cross_term = jnp.dot(left_pts, right_pts.T, preferred_element_type=jnp.float32)
    left_norm = jnp.sum(jnp.square(left_pts.astype(jnp.float32)), axis=1)
    right_norm = jnp.sum(jnp.square(right_pts.astype(jnp.float32)), axis=1)
    distance = left_norm[:, None] + right_norm[None, :] - 2.0 * cross_term
    return jnp.exp((-KERNEL_SCALE / left_pts.shape[1]) * distance)


def anterpolate(skel_x, rest_x, skel_w, rest_w):
    dense = kernel(skel_x, rest_x)
    spread = (dense / jnp.sum(dense, axis=0, keepdims=True)).astype(jnp.bfloat16)
    summed = skel_w.astype(jnp.float32) + jnp.dot(spread, rest_w, preferred_element_type=jnp.float32)
    return summed.astype(jnp.bfloat16)


def merge_node(payload):
    picked_x, picked_w = payload
    return picked_x[:SKEL], anterpolate(picked_x[:SKEL], picked_x[SKEL:], picked_w[:SKEL], picked_w[SKEL:])


def level_zero(payload):
    tree_x, tree_w, node_pick = payload
    return merge_node((tree_x[node_pick], tree_w[node_pick]))


def reference(points, weights, point_order, node_order, merge_order, far_list, task_target, task_source):
    features = points.shape[1]
    columns = weights.shape[1]
    devices = REGIONS * SLABS
    block_x = points.reshape(devices, PTS_DEV, features)
    block_w = weights.reshape(devices, PTS_DEV, columns)
    tree_order = point_order.reshape(devices, PTS_DEV)
    tree_x = jax.vmap(lambda rows_x, picks: rows_x[picks])(block_x, tree_order)
    tree_w = jax.vmap(lambda rows_w, picks: rows_w[picks])(block_w, tree_order)
    node_x, node_w = lax.map(level_zero, (tree_x, tree_w, node_order.reshape(devices, PTS_DEV)))
    node_x = node_x.reshape(REGIONS, SLABS, SKEL, features)
    node_w = node_w.reshape(REGIONS, SLABS, SKEL, columns)
    region = jnp.arange(REGIONS)
    sibling_x = []
    sibling_w = []
    for level_index in range(LEVELS):
        partner = region ^ (1 << level_index)
        other_x = node_x[partner]
        other_w = node_w[partner]
        sibling_x.append(other_x)
        sibling_w.append(other_w)
        if level_index < LEVELS - 1:
            upper = (((region >> level_index) & 1) == 1)[:, None, None, None]
            cat_x = jnp.concatenate([jnp.where(upper, other_x, node_x), jnp.where(upper, node_x, other_x)], axis=2)
            cat_w = jnp.concatenate([jnp.where(upper, other_w, node_w), jnp.where(upper, node_w, other_w)], axis=2)
            merge_rows = merge_order[:, :, level_index, :]
            picked_x = jnp.take_along_axis(cat_x, merge_rows[..., None], axis=2)
            picked_w = jnp.take_along_axis(cat_w, merge_rows[..., None], axis=2)
            new_x, new_w = lax.map(merge_node, (picked_x.reshape(devices, 2 * SKEL, features), picked_w.reshape(devices, 2 * SKEL, columns)))
            node_x = new_x.reshape(REGIONS, SLABS, SKEL, features)
            node_w = new_w.reshape(REGIONS, SLABS, SKEL, columns)
    stack_x = jnp.stack(sibling_x, axis=2).reshape(devices, LEVELS, SKEL, features)
    stack_w = jnp.stack(sibling_w, axis=2).reshape(devices, LEVELS, SKEL, columns)
    leaves_x = tree_x.reshape(REGIONS, SLABS, LEAF_DEV, LEAF_PTS, features)
    leaves_w = tree_w.reshape(REGIONS, SLABS, LEAF_DEV, LEAF_PTS, columns)
    far_flags = far_list.reshape(devices, LEAF_DEV, LEVELS)
    targets_all = task_target.reshape(devices, SLABS, CAP)
    sources_all = task_source.reshape(devices, SLABS, CAP)

    def pair_terms(payload):
        target_x, source_x, source_w = payload

        def single(one_t, one_s, one_w):
            return jnp.dot(kernel(one_t, one_s).astype(jnp.bfloat16), one_w, preferred_element_type=jnp.float32)

        return jax.vmap(single)(target_x, source_x, source_w)

    def device_sum(device):
        region_index = device // SLABS
        slab_index = device % SLABS
        own_x = tree_x[device]
        far_field = jnp.zeros((LEAF_DEV, LEAF_PTS, columns), jnp.float32)
        for level_index in range(LEVELS):
            dense = kernel(own_x, stack_x[device, level_index]).astype(jnp.bfloat16)
            far_part = jnp.dot(dense, stack_w[device, level_index], preferred_element_type=jnp.float32)
            flags = far_flags[device, :, level_index].astype(jnp.float32)
            far_field = far_field + far_part.reshape(LEAF_DEV, LEAF_PTS, columns) * flags[:, None, None]
        target = targets_all[device]
        source = sources_all[device]
        is_live = target >= 0
        slot_leaf = jnp.maximum(target, 0)
        own_leaves = leaves_x[region_index, slab_index]
        peer_rows = jnp.arange(SLABS)[:, None]
        chosen_x = leaves_x[region_index][peer_rows, source]
        chosen_w = leaves_w[region_index][peer_rows, source]
        slot_terms = lax.map(pair_terms, (own_leaves[slot_leaf], chosen_x, chosen_w))
        onehot = ((slot_leaf[..., None] == jnp.arange(LEAF_DEV)[None, None, :]) & is_live[..., None]).astype(jnp.float32)
        near_field = jnp.einsum('pcl,pcte->lte', onehot, slot_terms, precision=lax.Precision.HIGHEST)
        return (far_field + near_field).reshape(PTS_DEV, columns)

    result = lax.map(device_sum, jnp.arange(devices))
    return result.reshape(POINTS, columns)
```

```python
import functools
import math

import jax
import jax.numpy as jnp
from jax import lax
from jax.experimental import pallas as pl
from jax.experimental.pallas import tpu as pltpu
from jax.sharding import PartitionSpec as P

SKEL = 512
KERNEL_SCALE = 1.5
BF = jnp.bfloat16
F32 = jnp.float32

VMEM = pl.BlockSpec(memory_space=pltpu.VMEM)
SMEM = pl.BlockSpec(memory_space=pltpu.SMEM)


def partner(value, axis, stride):
    mask = 2**stride
    pairs = [(source, source ^ mask) for source in range(lax.axis_size(axis))]
    return lax.ppermute(value, axis, pairs)


def pieces(norm):
    first = norm.astype(BF).astype(F32)
    left = norm - first
    second = left.astype(BF).astype(F32)
    third = left - second
    return first, second, third


def row_norms(rows, features):
    width = rows.shape[1]
    square = rows * rows
    high = square.astype(BF)
    low = (square - high.astype(F32)).astype(BF)
    picks = (lax.broadcasted_iota(jnp.int32, (width, width), 0) < features).astype(F32).astype(BF)
    return jnp.dot(high, picks, preferred_element_type=F32) + jnp.dot(
        low, picks, preferred_element_type=F32
    )


def placed(lanes, features, body, parts, ones_first):
    first, second, third = parts
    a, b = (3, 0) if ones_first else (0, 3)
    out = jnp.where(lanes < features, body, 0.0)
    out = jnp.where(lanes == features + a, -first, out)
    out = jnp.where(lanes == features + a + 1, -second, out)
    out = jnp.where(lanes == features + a + 2, -third, out)
    ones = (lanes >= features + b) & (lanes < features + b + 3)
    return jnp.where(ones, 1.0, out).astype(BF)


def left_rows(rows, features):
    lanes = lax.broadcasted_iota(jnp.int32, rows.shape, 1)
    return placed(lanes, features, 2.0 * rows, pieces(row_norms(rows, features)), False)


def right_rows(rows, features):
    lanes = lax.broadcasted_iota(jnp.int32, rows.shape, 1)
    return placed(lanes, features, rows, pieces(row_norms(rows, features)), True)


NT = (((1,), (1,)), ((), ()))


def dense_of(exponent, features):
    return jnp.exp2(exponent * (KERNEL_SCALE / features * math.log2(math.e)))


def spread_of(exponent, features):
    dense = dense_of(exponent, features)
    return (dense * (1.0 / jnp.sum(dense, axis=0, keepdims=True))).astype(BF)


def turned(points_ref, weights_ref, rows_ref, extra_ref=None):
    step = 512
    for start in range(0, rows_ref.shape[0], step):
        both = jnp.concatenate(
            [points_ref[:, start : start + step], weights_ref[:, start : start + step]], axis=0
        )
        block = both.astype(F32).T
        rows_ref[start : start + step, :] = block
        if extra_ref is not None:
            extra_ref[start : start + step, :] = block


def level_zero_kernel(features, points_ref, weights_ref, order_ref, node_ref, out_ref,
                      rows_ref, rest_ref, skel_ref):
    count = points_ref.shape[1]
    turned(points_ref, weights_ref, rows_ref, rest_ref)
    blank = jnp.zeros((1, rows_ref.shape[1]), F32)
    group = 16

    def pick(step, carry):
        for inner in range(group):
            at = step * group + inner
            index = order_ref[node_ref[at]]
            skel_ref[pl.ds(at, 1), :] = rows_ref[pl.ds(index, 1), :]
            rest_ref[pl.ds(index, 1), :] = blank
        return carry

    lax.fori_loop(0, SKEL // group, pick, 0)
    skel = skel_ref[...]
    left = left_rows(skel, features)
    width = rows_ref.shape[1]
    chunk = 512
    total = jnp.zeros((SKEL, width), F32)
    for start in range(0, count, chunk):
        part = points_ref[:, start : start + chunk].astype(F32)
        norm = jnp.sum(part * part, axis=0, keepdims=True)
        first, second, third = pieces(norm)
        lines = lax.broadcasted_iota(jnp.int32, (width - features, chunk), 0)
        tail = jnp.where(lines < 3, 1.0, 0.0)
        tail = jnp.where(lines == 3, -first, tail)
        tail = jnp.where(lines == 4, -second, tail)
        tail = jnp.where(lines == 5, -third, tail)
        right = jnp.concatenate([part, tail], axis=0).astype(BF)
        spread = spread_of(jnp.dot(left, right, preferred_element_type=F32), features)
        total = total + jnp.dot(
            spread, rest_ref[start : start + chunk, :].astype(BF), preferred_element_type=F32
        )
    lanes = lax.broadcasted_iota(jnp.int32, (SKEL, width), 1)
    out_ref[...] = jnp.where(lanes < features, skel, skel + total).astype(BF)


def tree_kernel(points_ref, weights_ref, order_ref, wanted_ref, tree_ref, send_ref, rows_ref, picked_ref):
    turned(points_ref, weights_ref, rows_ref)
    group = 16

    def pick(step, carry):
        base = pl.multiple_of(step * group, group)
        for inner in range(group):
            index = order_ref[base + inner]
            picked_ref[pl.ds(base + inner, 1), :] = rows_ref[pl.ds(index, 1), :]
        return carry

    lax.fori_loop(0, tree_ref.shape[0] // group, pick, 0)
    tree_ref[...] = picked_ref[...].astype(BF)
    leaf = send_ref.shape[1]
    for slot in range(send_ref.shape[0]):
        begin = pl.multiple_of(wanted_ref[slot] * leaf, leaf)
        send_ref[slot] = tree_ref[pl.ds(begin, leaf), :]


def merge_kernel(features, upper_ref, own_ref, other_ref, order_ref, out_ref, rows_ref, rest_ref, skel_ref):
    width = own_ref.shape[1]
    own = own_ref[...].astype(F32)
    other = other_ref[...].astype(F32)
    rows_ref[:SKEL, :] = own
    rows_ref[SKEL:, :] = other
    rest_ref[:SKEL, :] = own
    rest_ref[SKEL:, :] = other
    blank = jnp.zeros((1, width), F32)
    flip = upper_ref[0] * SKEL
    group = 16

    def pick(step, carry):
        for inner in range(group):
            at = step * group + inner
            index = order_ref[at] ^ flip
            skel_ref[pl.ds(at, 1), :] = rows_ref[pl.ds(index, 1), :]
            rest_ref[pl.ds(index, 1), :] = blank
        return carry

    lax.fori_loop(0, SKEL // group, pick, 0)
    skel = skel_ref[...]
    left = left_rows(skel, features)
    total = jnp.zeros((SKEL, width), F32)
    chunk = 512
    for start in range(0, 2 * SKEL, chunk):
        right = right_rows(rows_ref[start : start + chunk, :], features)
        spread = spread_of(lax.dot_general(left, right, NT, preferred_element_type=F32), features)
        total = total + jnp.dot(
            spread, rest_ref[start : start + chunk, :].astype(BF), preferred_element_type=F32
        )
    lanes = lax.broadcasted_iota(jnp.int32, (SKEL, width), 1)
    out_ref[...] = jnp.where(lanes < features, skel, skel + total).astype(BF)


TILE = 256


def add_terms(features, left_ref, sum_ref, begin, leaf, right, value):
    def step(index, carry):
        at = pl.multiple_of(begin + index * TILE, TILE)
        exponent = lax.dot_general(
            left_ref[pl.ds(at, TILE), :], right, NT, preferred_element_type=F32
        )
        dense = dense_of(exponent, features).astype(BF)
        sum_ref[pl.ds(at, TILE), :] += jnp.dot(dense, value, preferred_element_type=F32)
        return carry

    lax.fori_loop(0, leaf // TILE, step, 0, unroll=True)


def far_terms(features, level, far_ref, node_ref, left_ref, sum_ref, leaf):
    value = node_ref[...]
    right = right_rows(value.astype(F32), features)
    for one in range(far_ref.shape[0]):
        @pl.when(far_ref[one, level] > 0)
        def _(one=one):
            add_terms(features, left_ref, sum_ref, one * leaf, leaf, right, value)


def start_kernel(features, far_ref, tree_ref, node_ref, left_ref, sum_ref):
    leaf = tree_ref.shape[0] // far_ref.shape[0]
    for start in range(0, tree_ref.shape[0], 512):
        left_ref[start : start + 512, :] = left_rows(
            tree_ref[start : start + 512, :].astype(F32), features
        )
    sum_ref[...] = jnp.zeros_like(sum_ref)
    far_terms(features, 0, far_ref, node_ref, left_ref, sum_ref, leaf)


def near_kernel(features, target_ref, near_ref, left_ref, prior_ref, sum_ref):
    leaf = near_ref.shape[1]
    sum_ref[...] = prior_ref[...]

    def one_slot(slot, carry):
        target = target_ref[slot]

        @pl.when(target >= 0)
        def _():
            begin = pl.multiple_of(target * leaf, leaf)
            for start in range(0, leaf, SKEL):
                value = near_ref[slot, start : start + SKEL, :]
                right = right_rows(value.astype(F32), features)
                add_terms(features, left_ref, sum_ref, begin, leaf, right, value)

        return carry

    lax.fori_loop(0, target_ref.shape[0], one_slot, 0)


def far_kernel(features, level, far_ref, node_ref, left_ref, prior_ref, sum_ref):
    leaf = left_ref.shape[0] // far_ref.shape[0]
    sum_ref[...] = prior_ref[...]
    far_terms(features, level, far_ref, node_ref, left_ref, sum_ref, leaf)


def last_kernel(features, level, far_ref, node_ref, left_ref, prior_ref, out_ref, sum_ref):
    leaf = left_ref.shape[0] // far_ref.shape[0]
    sum_ref[...] = prior_ref[...]
    far_terms(features, level, far_ref, node_ref, left_ref, sum_ref, leaf)
    for start in range(0, sum_ref.shape[0], 512):
        out_ref[:, start : start + 512] = sum_ref[start : start + 512, :].T[features:, :]


def cost(elements):
    return pl.CostEstimate(flops=elements * 512, transcendentals=elements, bytes_accessed=4 << 20)


PARAMS = pltpu.CompilerParams(vmem_limit_bytes=48 << 20)


def body(points, weights, point_order, node_order, merge_order, far_list, task_target, task_source):
    count, features = points.shape
    columns = weights.shape[1]
    width = features + columns
    levels = far_list.shape[3]
    leaves = far_list.shape[2]
    leaf = count // leaves
    slabs = task_source.shape[2]
    cap = task_source.shape[3]
    slots = slabs * cap
    points_t, weights_t = points.T, weights.T
    order = point_order[0, 0]
    far = far_list[0, 0]
    target = task_target[0, 0].reshape(slots)
    wanted = lax.all_to_all(task_source[0, 0], "task", split_axis=0, concat_axis=0, tiled=True)

    node = pl.pallas_call(
        functools.partial(level_zero_kernel, features),
        out_shape=jax.ShapeDtypeStruct((SKEL, width), BF),
        in_specs=[VMEM, VMEM, SMEM, SMEM],
        out_specs=VMEM,
        scratch_shapes=[
            pltpu.VMEM((count, width), F32),
            pltpu.VMEM((count, width), F32),
            pltpu.VMEM((SKEL, width), F32),
        ],
        cost_estimate=cost(SKEL * count),
        compiler_params=PARAMS,
        name="level_zero",
    )(points_t, weights_t, order, node_order[0, 0])

    tree, send = pl.pallas_call(
        tree_kernel,
        out_shape=(
            jax.ShapeDtypeStruct((count, width), BF),
            jax.ShapeDtypeStruct((slots, leaf, width), BF),
        ),
        in_specs=[VMEM, VMEM, SMEM, SMEM],
        out_specs=(VMEM, VMEM),
        scratch_shapes=[pltpu.VMEM((count, width), F32), pltpu.VMEM((count, width), F32)],
        cost_estimate=cost(SKEL * count),
        compiler_params=PARAMS,
        name="tree",
    )(points_t, weights_t, order, wanted.reshape(slots))
    arrived = lax.all_to_all(send, "task", split_axis=0, concat_axis=0, tiled=True)

    position = lax.axis_index("leaf")

    def merge(level, own, other):
        upper = (position >> level & 1).reshape(1)
        return pl.pallas_call(
            functools.partial(merge_kernel, features),
            out_shape=jax.ShapeDtypeStruct((SKEL, width), BF),
            in_specs=[SMEM, VMEM, VMEM, SMEM],
            out_specs=VMEM,
            scratch_shapes=[
                pltpu.VMEM((2 * SKEL, width), F32),
                pltpu.VMEM((2 * SKEL, width), F32),
                pltpu.VMEM((SKEL, width), F32),
            ],
            cost_estimate=cost(2 * SKEL * SKEL),
            compiler_params=PARAMS,
            name="merge",
        )(upper, own, other, merge_order[0, 0, level])

    siblings = []
    for level in range(levels):
        other = partner(node, "leaf", level)
        siblings.append(other)
        if level < levels - 1:
            node = merge(level, node, other)

    sums = jax.ShapeDtypeStruct((count, width), F32)
    left, total = pl.pallas_call(
        functools.partial(start_kernel, features),
        out_shape=(jax.ShapeDtypeStruct((count, width), BF), sums),
        in_specs=[SMEM, VMEM, VMEM],
        out_specs=(VMEM, VMEM),
        cost_estimate=cost(SKEL * count),
        compiler_params=PARAMS,
        name="far_first",
    )(far, tree, siblings[0])

    for level in range(1, levels - 1):
        total = pl.pallas_call(
            functools.partial(far_kernel, features, level),
            out_shape=sums,
            in_specs=[SMEM, VMEM, VMEM, VMEM],
            out_specs=VMEM,
            cost_estimate=cost(SKEL * count),
            compiler_params=PARAMS,
            name="far_middle",
        )(far, siblings[level], left, total)

    total = pl.pallas_call(
        functools.partial(near_kernel, features),
        out_shape=sums,
        in_specs=[SMEM, VMEM, VMEM, VMEM],
        out_specs=VMEM,
        cost_estimate=cost(slots * leaf * leaf),
        compiler_params=PARAMS,
        name="near",
    )(target, arrived, left, total)

    out = pl.pallas_call(
        functools.partial(last_kernel, features, levels - 1),
        out_shape=jax.ShapeDtypeStruct((columns, count), F32),
        in_specs=[SMEM, VMEM, VMEM, VMEM],
        out_specs=VMEM,
        scratch_shapes=[pltpu.VMEM((count, width), F32)],
        cost_estimate=cost(SKEL * count),
        compiler_params=PARAMS,
        name="far_last",
    )(far, siblings[levels - 1], left, total)
    return out.T


def solution(mesh):
    return jax.shard_map(
        body,
        mesh=mesh,
        in_specs=(
            P(("leaf", "task"), None),
            P(("leaf", "task"), None),
            P("leaf", "task", None),
            P("leaf", "task", None),
            P("leaf", "task", None, None),
            P("leaf", "task", None, None),
            P("leaf", "task", None, None),
            P("leaf", "task", None, None),
        ),
        out_specs=P(("leaf", "task"), None),
        check_vma=False,
    )
```

```python
import functools
import math

import jax
import jax.numpy as jnp
from jax import lax
from jax.experimental import pallas as pl
from jax.experimental.pallas import tpu as pltpu
from jax.sharding import PartitionSpec as P

SKEL = 512
KERNEL_SCALE = 1.5
BF = jnp.bfloat16
F32 = jnp.float32

VMEM = pl.BlockSpec(memory_space=pltpu.VMEM)
SMEM = pl.BlockSpec(memory_space=pltpu.SMEM)


def pieces(norm):
    first = norm.astype(BF).astype(F32)
    left = norm - first
    second = left.astype(BF).astype(F32)
    third = left - second
    return first, second, third


def row_norms(rows, features):
    width = rows.shape[1]
    square = rows * rows
    high = square.astype(BF)
    low = (square - high.astype(F32)).astype(BF)
    picks = (lax.broadcasted_iota(jnp.int32, (width, width), 0) < features).astype(F32).astype(BF)
    return jnp.dot(high, picks, preferred_element_type=F32) + jnp.dot(
        low, picks, preferred_element_type=F32
    )


def placed(lanes, features, body, parts, ones_first):
    first, second, third = parts
    a, b = (3, 0) if ones_first else (0, 3)
    out = jnp.where(lanes < features, body, 0.0)
    out = jnp.where(lanes == features + a, -first, out)
    out = jnp.where(lanes == features + a + 1, -second, out)
    out = jnp.where(lanes == features + a + 2, -third, out)
    ones = (lanes >= features + b) & (lanes < features + b + 3)
    return jnp.where(ones, 1.0, out).astype(BF)


def left_rows(rows, features):
    lanes = lax.broadcasted_iota(jnp.int32, rows.shape, 1)
    return placed(lanes, features, 2.0 * rows, pieces(row_norms(rows, features)), False)


def right_rows(rows, features):
    lanes = lax.broadcasted_iota(jnp.int32, rows.shape, 1)
    return placed(lanes, features, rows, pieces(row_norms(rows, features)), True)


NT = (((1,), (1,)), ((), ()))


def dense_of(exponent, features):
    return jnp.exp2(exponent * (KERNEL_SCALE / features * math.log2(math.e)))


def spread_of(exponent, features, kept):
    dense = dense_of(exponent, features)
    return (dense * (kept / jnp.sum(dense, axis=0, keepdims=True))).astype(BF)


def kept_columns(index_ref, start, count):
    step = index_ref.shape[1]
    found = []
    for base in range(start, start + count, step):
        lanes = lax.broadcasted_iota(jnp.int32, index_ref.shape, 1) + base
        hit = jnp.where(index_ref[...] == lanes, 0.0, 1.0)
        found.append(jnp.min(hit, axis=0, keepdims=True))
    return jnp.concatenate(found, axis=1)


def turned(points_ref, weights_ref, rows_ref):
    step = SKEL
    for start in range(0, rows_ref.shape[0], step):
        both = jnp.concatenate(
            [points_ref[:, start : start + step], weights_ref[:, start : start + step]], axis=0
        )
        rows_ref[start : start + step, :] = both.astype(F32).T


GROUP = 16


def pick_skeleton(index_of, rows_ref, skel_ref, index_ref):
    width = rows_ref.shape[1]

    def pick(step, carry):
        base = pl.multiple_of(step * GROUP, GROUP)
        for inner in range(GROUP):
            index = index_of(base + inner)
            skel_ref[pl.ds(base + inner, 1), :] = rows_ref[index][None]
            index_ref[pl.ds(base + inner, 1), :] = jnp.full((1, width), index, jnp.int32)
        return carry

    lax.fori_loop(0, SKEL // GROUP, pick, 0)


def with_total(skel, total, features):
    lanes = lax.broadcasted_iota(jnp.int32, skel.shape, 1)
    return jnp.where(lanes < features, skel, skel + total).astype(BF)


def level_zero(features, points_ref, rows_ref, skel_ref, index_ref):
    count = points_ref.shape[1]
    skel = skel_ref[...]
    left = left_rows(skel, features)
    width = rows_ref.shape[1]
    chunk = SKEL
    total = jnp.zeros((SKEL, width), F32)
    for start in range(0, count, chunk):
        part = points_ref[:, start : start + chunk].astype(F32)
        norm = jnp.sum(part * part, axis=0, keepdims=True)
        first, second, third = pieces(norm)
        lines = lax.broadcasted_iota(jnp.int32, (width - features, chunk), 0)
        tail = jnp.where(lines < 3, 1.0, 0.0)
        tail = jnp.where(lines == 3, -first, tail)
        tail = jnp.where(lines == 4, -second, tail)
        tail = jnp.where(lines == 5, -third, tail)
        right = jnp.concatenate([part, tail], axis=0).astype(BF)
        kept = kept_columns(index_ref, start, chunk)
        spread = spread_of(jnp.dot(left, right, preferred_element_type=F32), features, kept)
        total = total + jnp.dot(
            spread, rows_ref[start : start + chunk, :].astype(BF), preferred_element_type=F32
        )
    return with_total(skel, total, features)


def merged(features, rows_ref, skel_ref, index_ref):
    skel = skel_ref[...]
    left = left_rows(skel, features)
    total = jnp.zeros(skel.shape, F32)
    for start in range(0, 2 * SKEL, SKEL):
        rows = rows_ref[start : start + SKEL, :]
        right = right_rows(rows, features)
        exponent = lax.dot_general(left, right, NT, preferred_element_type=F32)
        spread = spread_of(exponent, features, kept_columns(index_ref, start, SKEL))
        total = total + jnp.dot(spread, rows.astype(BF), preferred_element_type=F32)
    return with_total(skel, total, features)


TILE = 256


def add_terms(features, left_ref, sum_ref, begin, leaf, right, value):
    def step(index, carry):
        at = pl.multiple_of(begin + index * TILE, TILE)
        exponent = lax.dot_general(
            left_ref[pl.ds(at, TILE), :], right, NT, preferred_element_type=F32
        )
        dense = dense_of(exponent, features).astype(BF)
        sum_ref[pl.ds(at, TILE), :] += jnp.dot(dense, value, preferred_element_type=F32)
        return carry

    lax.fori_loop(0, leaf // TILE, step, 0, unroll=True)


MESH = pl.DeviceIdType.MESH


def chain_kernel(features, levels, slabs, points_ref, weights_ref, order_ref, node_order_ref, merge_ref,
                 far_ref, source_ref, left_ref, sum_ref, near_ref, last_ref,
                 rows_ref, picked_ref, pair_ref, skel_ref, index_ref, node_ref, held_ref,
                 asked_ref, send_ref, node_send, node_recv, ask_send, ask_recv, near_send, near_recv):
    region = lax.axis_index("leaf")
    slab = lax.axis_index("task")
    count = rows_ref.shape[0]
    leaves = far_ref.shape[0]
    leaf = count // leaves
    cap = source_ref.shape[1]

    def bit(level):
        return region // 2**level % 2

    def sibling(level):
        return region + (1 - 2 * bit(level)) * 2**level

    def ahead(step):
        return lax.rem(slab + step, slabs)

    def behind(step):
        return lax.rem(slab + slabs - step, slabs)

    barrier = pltpu.get_barrier_semaphore()
    for level in range(levels):
        pl.semaphore_signal(barrier, inc=1, device_id=(sibling(level), slab), device_id_type=MESH)
    for step in range(1, slabs):
        pl.semaphore_signal(barrier, inc=1, device_id=(region, ahead(step)), device_id_type=MESH)

    turned(points_ref, weights_ref, rows_ref)
    pick_skeleton(lambda at: order_ref[node_order_ref[at]], rows_ref, skel_ref, index_ref)
    node_ref[0] = level_zero(features, points_ref, rows_ref, skel_ref, index_ref)

    pl.semaphore_wait(barrier, levels + slabs - 1)

    def node_copy(level):
        return pltpu.make_async_remote_copy(
            src_ref=node_ref.at[level],
            dst_ref=held_ref.at[level],
            send_sem=node_send.at[level],
            recv_sem=node_recv.at[level],
            device_id=(sibling(level), slab),
            device_id_type=MESH,
        )

    def ask_copy(step):
        return pltpu.make_async_remote_copy(
            src_ref=source_ref,
            dst_ref=asked_ref.at[step],
            send_sem=ask_send.at[step],
            recv_sem=ask_recv.at[step],
            device_id=(region, ahead(step)),
            device_id_type=MESH,
        )

    def near_copy(step):
        return pltpu.make_async_remote_copy(
            src_ref=send_ref.at[step],
            dst_ref=near_ref.at[step],
            send_sem=near_send.at[step],
            recv_sem=near_recv.at[step],
            device_id=(region, behind(step)),
            device_id_type=MESH,
        )

    node_copy(0).start()
    for step in range(1, slabs):
        ask_copy(step).start()

    def pick(step, carry):
        base = pl.multiple_of(step * GROUP, GROUP)
        for inner in range(GROUP):
            index = order_ref[base + inner]
            picked_ref[pl.ds(base + inner, 1), :] = rows_ref[index][None]
        return carry

    lax.fori_loop(0, count // GROUP, pick, 0)

    def fill(slot_ref, step, table):
        at_row = lax.broadcasted_iota(jnp.int32, table.shape, 0) == slab
        at_column = lax.broadcasted_iota(jnp.int32, table.shape, 1)
        for one in range(cap):
            wanted = jnp.max(
                jnp.where(at_row & (at_column == one), table, 0).astype(F32), axis=(0, 1), keepdims=True
            )
            for start in range(0, leaf, TILE):
                rows = picked_ref[start : start + TILE, :]
                for other in range(1, leaves):
                    begin = other * leaf + start
                    rows = jnp.where(wanted == other, picked_ref[begin : begin + TILE, :], rows)
                slot_ref[step, one * leaf + start : one * leaf + start + TILE, :] = rows.astype(BF)

    for step in range(1, slabs):
        ask_copy(step).wait_recv()
        fill(send_ref, step, asked_ref[step])
        near_copy(step).start()
    fill(near_ref, 0, source_ref[...])

    def far_terms(level):
        value = held_ref[level]
        right = right_rows(value.astype(F32), features)
        for one in range(leaves):
            flag = far_ref[one, level].astype(F32)
            weight = (value.astype(F32) * flag).astype(BF)
            add_terms(features, left_ref, sum_ref, one * leaf, leaf, right, weight)

    for level in range(levels):
        node_copy(level).wait_recv()
        if level == levels - 1:
            break
        upper = bit(level)
        pair_ref[pl.ds(pl.multiple_of(upper * SKEL, SKEL), SKEL), :] = node_ref[level].astype(F32)
        pair_ref[pl.ds(pl.multiple_of((1 - upper) * SKEL, SKEL), SKEL), :] = held_ref[level].astype(F32)
        pick_skeleton(lambda at: merge_ref[level, at], pair_ref, skel_ref, index_ref)
        node_ref[level + 1] = merged(features, pair_ref, skel_ref, index_ref)
        node_copy(level + 1).start()
        if level == 0:
            for start in range(0, count, SKEL):
                left_ref[start : start + SKEL, :] = left_rows(picked_ref[start : start + SKEL, :], features)
            sum_ref[...] = jnp.zeros_like(sum_ref)
        far_terms(level)
    last_ref[...] = held_ref[levels - 1]
    for level in range(levels):
        node_copy(level).wait_send()
    for step in range(1, slabs):
        ask_copy(step).wait_send()
        near_copy(step).wait_send()
        near_copy(step).wait_recv()


def last_kernel(features, level, slabs, slab_ref, far_ref, target_ref, node_ref, left_ref, near_ref,
                prior_ref, out_ref, sum_ref):
    leaves = far_ref.shape[0]
    leaf = left_ref.shape[0] // leaves
    sum_ref[...] = prior_ref[...]
    value = node_ref[...]
    right = right_rows(value.astype(F32), features)
    for one in range(leaves):
        @pl.when(far_ref[one, level] > 0)
        def _(one=one):
            add_terms(features, left_ref, sum_ref, one * leaf, leaf, right, value)

    def one_slab(step, carry):
        owner = lax.rem(slab_ref[0] + step, slabs)
        for one in range(target_ref.shape[1]):
            target = target_ref[owner, one]

            @pl.when(target >= 0)
            def _():
                begin = pl.multiple_of(target * leaf, leaf)
                for start in range(0, leaf, SKEL):
                    value = near_ref[step, one * leaf + start : one * leaf + start + SKEL, :]
                    right = right_rows(value.astype(F32), features)
                    add_terms(features, left_ref, sum_ref, begin, leaf, right, value)

        return carry

    lax.fori_loop(0, slabs, one_slab, 0)
    for start in range(0, sum_ref.shape[0], SKEL):
        out_ref[:, start : start + SKEL] = sum_ref[start : start + SKEL, :].T[features:, :]


def body(points, weights, point_order, node_order, merge_order, far_list, task_target, task_source):
    count, features = points.shape
    columns = weights.shape[1]
    width = features + columns
    levels = far_list.shape[3]
    leaf = count // far_list.shape[2]
    slabs, cap = task_source.shape[2:]
    far = far_list[0, 0]
    source = task_source[0, 0]
    left, total, near, last = pl.pallas_call(
        functools.partial(chain_kernel, features, levels, slabs),
        out_shape=(
            jax.ShapeDtypeStruct((count, width), BF),
            jax.ShapeDtypeStruct((count, width), F32),
            jax.ShapeDtypeStruct((slabs, cap * leaf, width), BF),
            jax.ShapeDtypeStruct((SKEL, width), BF),
        ),
        in_specs=[VMEM, VMEM, SMEM, SMEM, SMEM, SMEM, VMEM],
        out_specs=(VMEM, VMEM, VMEM, VMEM),
        scratch_shapes=[
            pltpu.VMEM((count, width), F32),
            pltpu.VMEM((count, width), F32),
            pltpu.VMEM((2 * SKEL, width), F32),
            pltpu.VMEM((SKEL, width), F32),
            pltpu.VMEM((SKEL, width), jnp.int32),
            pltpu.VMEM((levels, SKEL, width), BF),
            pltpu.VMEM((levels, SKEL, width), BF),
            pltpu.VMEM((slabs, slabs, cap), jnp.int32),
            pltpu.VMEM((slabs, cap * leaf, width), BF),
            pltpu.SemaphoreType.DMA((levels,)),
            pltpu.SemaphoreType.DMA((levels,)),
            pltpu.SemaphoreType.DMA((slabs,)),
            pltpu.SemaphoreType.DMA((slabs,)),
            pltpu.SemaphoreType.DMA((slabs,)),
            pltpu.SemaphoreType.DMA((slabs,)),
        ],
        compiler_params=pltpu.CompilerParams(
            collective_id=0, has_side_effects=True, vmem_limit_bytes=48 << 20
        ),
        name="chain",
    )(points.T, weights.T, point_order[0, 0], node_order[0, 0], merge_order[0, 0], far, source)
    slab = lax.axis_index("task").reshape(1)
    out = pl.pallas_call(
        functools.partial(last_kernel, features, levels - 1, slabs),
        out_shape=jax.ShapeDtypeStruct((columns, count), F32),
        in_specs=[SMEM, SMEM, SMEM, VMEM, VMEM, VMEM, VMEM],
        out_specs=VMEM,
        scratch_shapes=[pltpu.VMEM((count, width), F32)],
        compiler_params=pltpu.CompilerParams(vmem_limit_bytes=48 << 20),
        name="near_and_last",
    )(slab, far, task_target[0, 0], last, left, near, total)
    return out.T


def solution(mesh):
    return jax.shard_map(
        body,
        mesh=mesh,
        in_specs=(
            P(("leaf", "task"), None),
            P(("leaf", "task"), None),
            P("leaf", "task", None),
            P("leaf", "task", None),
            P("leaf", "task", None, None),
            P("leaf", "task", None, None),
            P("leaf", "task", None, None),
            P("leaf", "task", None, None),
        ),
        out_specs=P(("leaf", "task"), None),
        check_vma=False,
    )
```

```python
import functools
import math

import jax
import jax.numpy as jnp
from jax import lax
from jax.experimental import pallas as pl
from jax.experimental.pallas import tpu as pltpu
from jax.sharding import PartitionSpec as P

SKEL = 512
KERNEL_SCALE = 1.5
BF = jnp.bfloat16
F32 = jnp.float32

VMEM = pl.BlockSpec(memory_space=pltpu.VMEM)
SMEM = pl.BlockSpec(memory_space=pltpu.SMEM)
HBM = pl.BlockSpec(memory_space=pltpu.HBM)


def pieces(norm):
    first = norm.astype(BF).astype(F32)
    left = norm - first
    second = left.astype(BF).astype(F32)
    third = left - second
    return first, second, third


def row_norms(rows, features):
    width = rows.shape[1]
    square = rows * rows
    high = square.astype(BF)
    low = (square - high.astype(F32)).astype(BF)
    picks = (lax.broadcasted_iota(jnp.int32, (width, width), 0) < features).astype(F32).astype(BF)
    return jnp.dot(high, picks, preferred_element_type=F32) + jnp.dot(
        low, picks, preferred_element_type=F32
    )


def placed(lanes, features, body, parts, ones_first):
    first, second, third = parts
    a, b = (3, 0) if ones_first else (0, 3)
    out = jnp.where(lanes < features, body, 0.0)
    out = jnp.where(lanes == features + a, -first, out)
    out = jnp.where(lanes == features + a + 1, -second, out)
    out = jnp.where(lanes == features + a + 2, -third, out)
    ones = (lanes >= features + b) & (lanes < features + b + 3)
    return jnp.where(ones, 1.0, out).astype(BF)


def left_rows(rows, features):
    lanes = lax.broadcasted_iota(jnp.int32, rows.shape, 1)
    return placed(lanes, features, 2.0 * rows, pieces(row_norms(rows, features)), False)


def right_rows(rows, features):
    lanes = lax.broadcasted_iota(jnp.int32, rows.shape, 1)
    return placed(lanes, features, rows, pieces(row_norms(rows, features)), True)


NT = (((1,), (1,)), ((), ()))


def dense_of(exponent, features):
    return jnp.exp2(exponent * (KERNEL_SCALE / features * math.log2(math.e)))


def spread_of(exponent, features, kept):
    dense = dense_of(exponent, features)
    return (dense * (kept / jnp.sum(dense, axis=0, keepdims=True))).astype(BF)


def kept_columns(index_ref, start, count):
    step = index_ref.shape[1]
    found = []
    for base in range(start, start + count, step):
        lanes = lax.broadcasted_iota(jnp.int32, index_ref.shape, 1) + base
        hit = jnp.where(index_ref[...] == lanes, 0.0, 1.0)
        found.append(jnp.min(hit, axis=0, keepdims=True))
    return jnp.concatenate(found, axis=1)


def turned(points_ref, weights_ref, rows_ref):
    step = SKEL
    for start in range(0, rows_ref.shape[0], step):
        both = jnp.concatenate(
            [points_ref[:, start : start + step], weights_ref[:, start : start + step]], axis=0
        )
        rows_ref[start : start + step, :] = both.astype(F32).T


GROUP = 16


def pick_skeleton(index_of, rows_ref, skel_ref, index_ref):
    width = rows_ref.shape[1]

    def pick(step, carry):
        base = pl.multiple_of(step * GROUP, GROUP)
        for inner in range(GROUP):
            index = index_of(base + inner)
            skel_ref[pl.ds(base + inner, 1), :] = rows_ref[index][None]
            index_ref[pl.ds(base + inner, 1), :] = jnp.full((1, width), index, jnp.int32)
        return carry

    lax.fori_loop(0, SKEL // GROUP, pick, 0)


def with_total(skel, total, features):
    lanes = lax.broadcasted_iota(jnp.int32, skel.shape, 1)
    return jnp.where(lanes < features, skel, skel + total).astype(BF)


def level_zero(features, points_ref, rows_ref, skel_ref, index_ref):
    count = points_ref.shape[1]
    skel = skel_ref[...]
    left = left_rows(skel, features)
    width = rows_ref.shape[1]
    chunk = SKEL
    total = jnp.zeros((SKEL, width), F32)
    for start in range(0, count, chunk):
        part = points_ref[:, start : start + chunk].astype(F32)
        norm = jnp.sum(part * part, axis=0, keepdims=True)
        first, second, third = pieces(norm)
        lines = lax.broadcasted_iota(jnp.int32, (width - features, chunk), 0)
        tail = jnp.where(lines < 3, 1.0, 0.0)
        tail = jnp.where(lines == 3, -first, tail)
        tail = jnp.where(lines == 4, -second, tail)
        tail = jnp.where(lines == 5, -third, tail)
        right = jnp.concatenate([part, tail], axis=0).astype(BF)
        kept = kept_columns(index_ref, start, chunk)
        spread = spread_of(jnp.dot(left, right, preferred_element_type=F32), features, kept)
        total = total + jnp.dot(
            spread, rows_ref[start : start + chunk, :].astype(BF), preferred_element_type=F32
        )
    return with_total(skel, total, features)


def merged(features, rows_ref, skel_ref, index_ref):
    skel = skel_ref[...]
    left = left_rows(skel, features)
    total = jnp.zeros(skel.shape, F32)
    for start in range(0, 2 * SKEL, SKEL):
        rows = rows_ref[start : start + SKEL, :]
        right = right_rows(rows, features)
        exponent = lax.dot_general(left, right, NT, preferred_element_type=F32)
        spread = spread_of(exponent, features, kept_columns(index_ref, start, SKEL))
        total = total + jnp.dot(spread, rows.astype(BF), preferred_element_type=F32)
    return with_total(skel, total, features)


TILE = 256


FAR_TILE = 1024


def add_terms(features, left_ref, sum_ref, begin, leaf, right, value):
    tile = min(FAR_TILE, leaf)

    def step(index, carry):
        at = pl.multiple_of(begin + index * tile, tile)
        exponent = lax.dot_general(
            left_ref[pl.ds(at, tile), :], right, NT, preferred_element_type=F32
        )
        dense = dense_of(exponent, features).astype(BF)
        sum_ref[pl.ds(at, tile), :] += jnp.dot(dense, value, preferred_element_type=F32)
        return carry

    lax.fori_loop(0, leaf // tile, step, 0, unroll=True)


MESH = pl.DeviceIdType.MESH


def chain_kernel(features, levels, slabs, points_in, weights_in, order_in, node_order_in, merge_in,
                 far_in, source_in, left_ref, sum_ref, near_ref, last_ref,
                 rows_ref, picked_ref, pair_ref, skel_ref, index_ref, node_ref, held_ref,
                 asked_ref, send_ref, points_ref, weights_ref, order_ref, node_order_ref,
                 merge_ref, far_ref, source_ref, input_sem, node_send, node_recv, ask_send, ask_recv, near_send, near_recv):
    loads = [
        pltpu.make_async_copy(source, target, input_sem.at[at])
        for at, (source, target) in enumerate([
            (points_in, points_ref),
            (weights_in, weights_ref),
            (order_in, order_ref),
            (node_order_in, node_order_ref),
            (merge_in, merge_ref),
            (far_in, far_ref),
            (source_in, source_ref),
        ])
    ]
    for load in loads:
        load.start()
    region = lax.axis_index("leaf")
    slab = lax.axis_index("task")
    count = rows_ref.shape[0]
    leaves = far_ref.shape[2]
    leaf = count // leaves
    cap = source_ref.shape[0]

    def bit(level):
        return region // 2**level % 2

    def sibling(level):
        return region + (1 - 2 * bit(level)) * 2**level

    def ahead(step):
        return lax.rem(slab + step, slabs)

    def behind(step):
        return lax.rem(slab + slabs - step, slabs)

    barrier = pltpu.get_barrier_semaphore()
    for level in range(levels):
        pl.semaphore_signal(barrier, inc=1, device_id=(sibling(level), slab), device_id_type=MESH)
    for step in range(1, slabs):
        pl.semaphore_signal(barrier, inc=1, device_id=(region, ahead(step)), device_id_type=MESH)

    for load in loads:
        load.wait()
    turned(points_ref, weights_ref, rows_ref)
    pick_skeleton(lambda at: order_ref[node_order_ref[at]], rows_ref, skel_ref, index_ref)
    node_ref[0] = level_zero(features, points_ref, rows_ref, skel_ref, index_ref)

    pl.semaphore_wait(barrier, levels + slabs - 1)

    def node_copy(level):
        return pltpu.make_async_remote_copy(
            src_ref=node_ref.at[level],
            dst_ref=held_ref.at[level],
            send_sem=node_send.at[level],
            recv_sem=node_recv.at[level],
            device_id=(sibling(level), slab),
            device_id_type=MESH,
        )

    def ask_copy(step):
        return pltpu.make_async_remote_copy(
            src_ref=source_ref,
            dst_ref=asked_ref.at[step],
            send_sem=ask_send.at[step],
            recv_sem=ask_recv.at[step],
            device_id=(region, ahead(step)),
            device_id_type=MESH,
        )

    def near_copy(step):
        return pltpu.make_async_remote_copy(
            src_ref=send_ref.at[step],
            dst_ref=near_ref.at[step],
            send_sem=near_send.at[step],
            recv_sem=near_recv.at[step],
            device_id=(region, behind(step)),
            device_id_type=MESH,
        )

    node_copy(0).start()
    for step in range(1, slabs):
        ask_copy(step).start()

    def pick(step, carry):
        base = pl.multiple_of(step * GROUP, GROUP)
        for inner in range(GROUP):
            index = order_ref[base + inner]
            picked_ref[pl.ds(base + inner, 1), :] = rows_ref[index][None]
        return carry

    lax.fori_loop(0, count // GROUP, pick, 0)

    def fill(slot_ref, step, table):
        own = lax.broadcasted_iota(jnp.int32, table.shape, 1) == slab
        place = lax.broadcasted_iota(jnp.int32, table.shape, 0)
        for one in range(cap):
            wanted = jnp.max(
                jnp.where(own & (place == one), table, 0).astype(F32), axis=(0, 1), keepdims=True
            )
            for start in range(0, leaf, TILE):
                rows = picked_ref[start : start + TILE, :]
                for other in range(1, leaves):
                    begin = other * leaf + start
                    rows = jnp.where(wanted == other, picked_ref[begin : begin + TILE, :], rows)
                slot_ref[step, one * leaf + start : one * leaf + start + TILE, :] = rows.astype(BF)

    for step in range(1, slabs):
        ask_copy(step).wait_recv()
        fill(send_ref, step, asked_ref[step])
        near_copy(step).start()
    fill(near_ref, 0, source_ref[...])

    def far_terms(level):
        value = held_ref[level]
        right = right_rows(value.astype(F32), features)
        for one in range(leaves):
            flag = far_ref[level, 0, one].astype(F32)
            weight = (value.astype(F32) * flag).astype(BF)
            add_terms(features, left_ref, sum_ref, one * leaf, leaf, right, weight)

    for level in range(levels):
        node_copy(level).wait_recv()
        if level == levels - 1:
            break
        upper = bit(level)
        pair_ref[pl.ds(pl.multiple_of(upper * SKEL, SKEL), SKEL), :] = node_ref[level].astype(F32)
        pair_ref[pl.ds(pl.multiple_of((1 - upper) * SKEL, SKEL), SKEL), :] = held_ref[level].astype(F32)
        pick_skeleton(lambda at: merge_ref[level, at], pair_ref, skel_ref, index_ref)
        node_ref[level + 1] = merged(features, pair_ref, skel_ref, index_ref)
        node_copy(level + 1).start()
        if level == 0:
            for start in range(0, count, SKEL):
                left_ref[start : start + SKEL, :] = left_rows(picked_ref[start : start + SKEL, :], features)
            sum_ref[...] = jnp.zeros_like(sum_ref)
        far_terms(level)
    last_ref[...] = held_ref[levels - 1]
    for level in range(levels):
        node_copy(level).wait_send()
    for step in range(1, slabs):
        ask_copy(step).wait_send()
        near_copy(step).wait_send()
        near_copy(step).wait_recv()


def last_kernel(features, level, slabs, far_in, target_in, node_ref, left_ref, near_ref,
                prior_ref, out_ref, sum_ref, far_ref, target_ref, input_sem):
    loads = [
        pltpu.make_async_copy(far_in, far_ref, input_sem.at[0]),
        pltpu.make_async_copy(target_in, target_ref, input_sem.at[1]),
    ]
    for load in loads:
        load.start()
    leaves = far_ref.shape[2]
    leaf = left_ref.shape[0] // leaves
    sum_ref[...] = prior_ref[...]
    value = node_ref[...]
    right = right_rows(value.astype(F32), features)
    for load in loads:
        load.wait()
    for one in range(leaves):
        @pl.when(far_ref[level, 0, one] > 0)
        def _(one=one):
            add_terms(features, left_ref, sum_ref, one * leaf, leaf, right, value)

    def one_slab(step, carry):
        owner = lax.rem(lax.axis_index("task") + step, slabs)
        for one in range(target_ref.shape[0]):
            target = target_ref[one, owner]

            @pl.when(target >= 0)
            def _():
                begin = pl.multiple_of(target * leaf, leaf)
                for start in range(0, leaf, SKEL):
                    value = near_ref[step, one * leaf + start : one * leaf + start + SKEL, :]
                    right = right_rows(value.astype(F32), features)
                    add_terms(features, left_ref, sum_ref, begin, leaf, right, value)

        return carry

    lax.fori_loop(0, slabs, one_slab, 0)
    for start in range(0, sum_ref.shape[0], SKEL):
        out_ref[:, start : start + SKEL] = sum_ref[start : start + SKEL, :].T[features:, :]


def in_hbm(value):
    return pltpu.with_memory_space_constraint(value, pltpu.HBM)


def body(points, weights, point_order, node_order, merge_order, far_list, task_target, task_source):
    count, features = points.shape
    columns = weights.shape[1]
    width = features + columns
    levels = far_list.shape[3]
    leaf = count // far_list.shape[2]
    slabs, cap = task_source.shape[2:]
    far = far_list.transpose(0, 3, 1, 2)[0]
    source = task_source[0, 0].T
    inputs = (points.T, weights.T, point_order[0, 0], node_order[0, 0], merge_order[0, 0], far, source)
    left, total, near, last = pl.pallas_call(
        functools.partial(chain_kernel, features, levels, slabs),
        out_shape=(
            jax.ShapeDtypeStruct((count, width), BF),
            jax.ShapeDtypeStruct((count, width), F32),
            jax.ShapeDtypeStruct((slabs, cap * leaf, width), BF),
            jax.ShapeDtypeStruct((SKEL, width), BF),
        ),
        in_specs=[HBM] * 7,
        out_specs=(VMEM, VMEM, VMEM, VMEM),
        scratch_shapes=[
            pltpu.VMEM((count, width), F32),
            pltpu.VMEM((count, width), F32),
            pltpu.VMEM((2 * SKEL, width), F32),
            pltpu.VMEM((SKEL, width), F32),
            pltpu.VMEM((SKEL, width), jnp.int32),
            pltpu.VMEM((levels, SKEL, width), BF),
            pltpu.VMEM((levels, SKEL, width), BF),
            pltpu.VMEM((slabs, cap, slabs), jnp.int32),
            pltpu.VMEM((slabs, cap * leaf, width), BF),
            pltpu.VMEM((features, count), BF),
            pltpu.VMEM((columns, count), BF),
            pltpu.SMEM((count,), jnp.int32),
            pltpu.SMEM((count,), jnp.int32),
            pltpu.SMEM((levels - 1, 2 * SKEL), jnp.int32),
            pltpu.SMEM(far.shape, jnp.int32),
            pltpu.VMEM(source.shape, jnp.int32),
            pltpu.SemaphoreType.DMA((7,)),
            pltpu.SemaphoreType.DMA((levels,)),
            pltpu.SemaphoreType.DMA((levels,)),
            pltpu.SemaphoreType.DMA((slabs,)),
            pltpu.SemaphoreType.DMA((slabs,)),
            pltpu.SemaphoreType.DMA((slabs,)),
            pltpu.SemaphoreType.DMA((slabs,)),
        ],
        compiler_params=pltpu.CompilerParams(
            collective_id=0, has_side_effects=True, vmem_limit_bytes=48 << 20
        ),
        name="chain",
    )(*[in_hbm(one) for one in inputs])
    target = task_target[0, 0].T
    out = pl.pallas_call(
        functools.partial(last_kernel, features, levels - 1, slabs),
        out_shape=jax.ShapeDtypeStruct((columns, count), F32),
        in_specs=[HBM, HBM, VMEM, VMEM, VMEM, VMEM],
        out_specs=VMEM,
        scratch_shapes=[
            pltpu.VMEM((count, width), F32),
            pltpu.SMEM(far.shape, jnp.int32),
            pltpu.SMEM(target.shape, jnp.int32),
            pltpu.SemaphoreType.DMA((2,)),
        ],
        compiler_params=pltpu.CompilerParams(vmem_limit_bytes=48 << 20),
        name="near_and_last",
    )(in_hbm(far), in_hbm(target), last, left, near, total)
    return out.T


def solution(mesh):
    return jax.shard_map(
        body,
        mesh=mesh,
        in_specs=(
            P(("leaf", "task"), None),
            P(("leaf", "task"), None),
            P("leaf", "task", None),
            P("leaf", "task", None),
            P("leaf", "task", None, None),
            P("leaf", "task", None, None),
            P("leaf", "task", None, None),
            P("leaf", "task", None, None),
        ),
        out_specs=P(("leaf", "task"), None),
        check_vma=False,
    )
```

```python
import functools
import math

import jax
import jax.numpy as jnp
from jax import lax
from jax.experimental import pallas as pl
from jax.experimental.pallas import tpu as pltpu
from jax.sharding import PartitionSpec as P

SKEL = 512
KERNEL_SCALE = 1.5
BF = jnp.bfloat16
F32 = jnp.float32

VMEM = pl.BlockSpec(memory_space=pltpu.VMEM)
SMEM = pl.BlockSpec(memory_space=pltpu.SMEM)
HBM = pl.BlockSpec(memory_space=pltpu.HBM)


def pieces(norm):
    first = norm.astype(BF).astype(F32)
    left = norm - first
    second = left.astype(BF).astype(F32)
    third = left - second
    return first, second, third


def row_norms(rows, features):
    width = rows.shape[1]
    square = rows * rows
    high = square.astype(BF)
    low = (square - high.astype(F32)).astype(BF)
    picks = (lax.broadcasted_iota(jnp.int32, (width, width), 0) < features).astype(F32).astype(BF)
    return jnp.dot(high, picks, preferred_element_type=F32) + jnp.dot(
        low, picks, preferred_element_type=F32
    )


def placed(lanes, features, body, parts, ones_first):
    first, second, third = parts
    a, b = (3, 0) if ones_first else (0, 3)
    out = jnp.where(lanes < features, body, 0.0)
    out = jnp.where(lanes == features + a, -first, out)
    out = jnp.where(lanes == features + a + 1, -second, out)
    out = jnp.where(lanes == features + a + 2, -third, out)
    ones = (lanes >= features + b) & (lanes < features + b + 3)
    return jnp.where(ones, 1.0, out).astype(BF)


def left_rows(rows, features):
    lanes = lax.broadcasted_iota(jnp.int32, rows.shape, 1)
    return placed(lanes, features, 2.0 * rows, pieces(row_norms(rows, features)), False)


def right_rows(rows, features):
    lanes = lax.broadcasted_iota(jnp.int32, rows.shape, 1)
    return placed(lanes, features, rows, pieces(row_norms(rows, features)), True)


NT = (((1,), (1,)), ((), ()))


def dense_of(exponent, features):
    return jnp.exp2(exponent * (KERNEL_SCALE / features * math.log2(math.e)))


def spread_of(exponent, features, kept):
    dense = dense_of(exponent, features)
    return (dense * (kept / jnp.sum(dense, axis=0, keepdims=True))).astype(BF)


def kept_columns(index_ref, start, count):
    step = index_ref.shape[1]
    found = []
    for base in range(start, start + count, step):
        lanes = lax.broadcasted_iota(jnp.int32, index_ref.shape, 1) + base
        hit = jnp.where(index_ref[...] == lanes, 0.0, 1.0)
        found.append(jnp.min(hit, axis=0, keepdims=True))
    return jnp.concatenate(found, axis=1)


def turned(points_ref, weights_ref, rows_ref):
    step = SKEL
    for start in range(0, rows_ref.shape[0], step):
        both = jnp.concatenate(
            [points_ref[:, start : start + step], weights_ref[:, start : start + step]], axis=0
        )
        rows_ref[start : start + step, :] = both.astype(F32).T


GROUP = 32


def pick_skeleton(index_of, rows_ref, skel_ref, index_ref):
    width = rows_ref.shape[1]

    def pick(step, carry):
        base = pl.multiple_of(step * GROUP, GROUP)
        found = [index_of(base + inner) for inner in range(GROUP)]
        rows = [rows_ref[index][None] for index in found]
        for inner, (index, row) in enumerate(zip(found, rows)):
            skel_ref[pl.ds(base + inner, 1), :] = row
            index_ref[pl.ds(base + inner, 1), :] = jnp.full((1, width), index, jnp.int32)
        return carry

    lax.fori_loop(0, SKEL // GROUP, pick, 0)


def with_total(skel, total, features):
    lanes = lax.broadcasted_iota(jnp.int32, skel.shape, 1)
    return jnp.where(lanes < features, skel, skel + total).astype(BF)


def level_zero(features, points_ref, rows_ref, skel_ref, index_ref):
    count = points_ref.shape[1]
    skel = skel_ref[...]
    left = left_rows(skel, features)
    width = rows_ref.shape[1]
    chunk = SKEL
    total = jnp.zeros((SKEL, width), F32)
    for start in range(0, count, chunk):
        part = points_ref[:, start : start + chunk].astype(F32)
        norm = jnp.sum(part * part, axis=0, keepdims=True)
        first, second, third = pieces(norm)
        lines = lax.broadcasted_iota(jnp.int32, (width - features, chunk), 0)
        tail = jnp.where(lines < 3, 1.0, 0.0)
        tail = jnp.where(lines == 3, -first, tail)
        tail = jnp.where(lines == 4, -second, tail)
        tail = jnp.where(lines == 5, -third, tail)
        right = jnp.concatenate([part, tail], axis=0).astype(BF)
        kept = kept_columns(index_ref, start, chunk)
        spread = spread_of(jnp.dot(left, right, preferred_element_type=F32), features, kept)
        total = total + jnp.dot(
            spread, rows_ref[start : start + chunk, :].astype(BF), preferred_element_type=F32
        )
    return with_total(skel, total, features)


def merged(features, rows_ref, skel_ref, index_ref):
    skel = skel_ref[...]
    left = left_rows(skel, features)
    total = jnp.zeros(skel.shape, F32)
    for start in range(0, 2 * SKEL, SKEL):
        rows = rows_ref[start : start + SKEL, :]
        right = right_rows(rows, features)
        exponent = lax.dot_general(left, right, NT, preferred_element_type=F32)
        spread = spread_of(exponent, features, kept_columns(index_ref, start, SKEL))
        total = total + jnp.dot(spread, rows.astype(BF), preferred_element_type=F32)
    return with_total(skel, total, features)


TILE = 256


FAR_TILE = 1024


def add_terms(features, left_ref, sum_ref, begin, leaf, right, value):
    tile = min(FAR_TILE, leaf)

    def step(index, carry):
        at = pl.multiple_of(begin + index * tile, tile)
        exponent = lax.dot_general(
            left_ref[pl.ds(at, tile), :], right, NT, preferred_element_type=F32
        )
        dense = dense_of(exponent, features).astype(BF)
        sum_ref[pl.ds(at, tile), :] += jnp.dot(dense, value, preferred_element_type=F32)
        return carry

    lax.fori_loop(0, leaf // tile, step, 0, unroll=True)


MESH = pl.DeviceIdType.MESH


def chain_kernel(features, levels, slabs, points_in, weights_in, order_in, node_order_in, merge_in,
                 far_in, source_in, left_ref, sum_ref, near_ref, last_ref,
                 rows_ref, picked_ref, pair_ref, skel_ref, index_ref, node_ref, held_ref,
                 asked_ref, send_ref, points_ref, weights_ref, order_ref, node_order_ref,
                 merge_ref, far_ref, source_ref, input_sem, node_send, node_recv, ask_send, ask_recv, near_send, near_recv):
    loads = [
        pltpu.make_async_copy(source, target, input_sem.at[at])
        for at, (source, target) in enumerate([
            (points_in, points_ref),
            (weights_in, weights_ref),
            (order_in, order_ref),
            (node_order_in, node_order_ref),
            (merge_in, merge_ref),
            (far_in, far_ref),
            (source_in, source_ref),
        ])
    ]
    for load in loads:
        load.start()
    region = lax.axis_index("leaf")
    slab = lax.axis_index("task")
    count = rows_ref.shape[0]
    leaves = far_ref.shape[2]
    leaf = count // leaves
    cap = source_ref.shape[0]

    def bit(level):
        return region // 2**level % 2

    def sibling(level):
        return region + (1 - 2 * bit(level)) * 2**level

    def ahead(step):
        return lax.rem(slab + step, slabs)

    def behind(step):
        return lax.rem(slab + slabs - step, slabs)

    barrier = pltpu.get_barrier_semaphore()
    for level in range(levels):
        pl.semaphore_signal(barrier, inc=1, device_id=(sibling(level), slab), device_id_type=MESH)
    for step in range(1, slabs):
        pl.semaphore_signal(barrier, inc=1, device_id=(region, ahead(step)), device_id_type=MESH)

    for load in loads:
        load.wait()
    turned(points_ref, weights_ref, rows_ref)
    pick_skeleton(lambda at: order_ref[node_order_ref[at]], rows_ref, skel_ref, index_ref)
    node_ref[0] = level_zero(features, points_ref, rows_ref, skel_ref, index_ref)

    pl.semaphore_wait(barrier, levels + slabs - 1)

    def node_copy(level):
        return pltpu.make_async_remote_copy(
            src_ref=node_ref.at[level],
            dst_ref=held_ref.at[level],
            send_sem=node_send.at[level],
            recv_sem=node_recv.at[level],
            device_id=(sibling(level), slab),
            device_id_type=MESH,
        )

    def ask_copy(step):
        return pltpu.make_async_remote_copy(
            src_ref=source_ref,
            dst_ref=asked_ref.at[step],
            send_sem=ask_send.at[step],
            recv_sem=ask_recv.at[step],
            device_id=(region, ahead(step)),
            device_id_type=MESH,
        )

    def near_copy(step):
        return pltpu.make_async_remote_copy(
            src_ref=send_ref.at[step],
            dst_ref=near_ref.at[step],
            send_sem=near_send.at[step],
            recv_sem=near_recv.at[step],
            device_id=(region, behind(step)),
            device_id_type=MESH,
        )

    node_copy(0).start()
    for step in range(1, slabs):
        ask_copy(step).start()

    def pick(step, carry):
        base = pl.multiple_of(step * GROUP, GROUP)
        rows = [rows_ref[order_ref[base + inner]][None] for inner in range(GROUP)]
        for inner, row in enumerate(rows):
            picked_ref[pl.ds(base + inner, 1), :] = row
        return carry

    lax.fori_loop(0, count // GROUP, pick, 0)

    def fill(slot_ref, step, table):
        own = lax.broadcasted_iota(jnp.int32, table.shape, 1) == slab
        place = lax.broadcasted_iota(jnp.int32, table.shape, 0)
        for one in range(cap):
            wanted = jnp.max(
                jnp.where(own & (place == one), table, 0).astype(F32), axis=(0, 1), keepdims=True
            )
            for start in range(0, leaf, TILE):
                rows = picked_ref[start : start + TILE, :]
                for other in range(1, leaves):
                    begin = other * leaf + start
                    rows = jnp.where(wanted == other, picked_ref[begin : begin + TILE, :], rows)
                slot_ref[step, one * leaf + start : one * leaf + start + TILE, :] = rows.astype(BF)

    for step in range(1, slabs):
        ask_copy(step).wait_recv()
        fill(send_ref, step, asked_ref[step])
        near_copy(step).start()
    fill(near_ref, 0, source_ref[...])

    def far_terms(level):
        value = held_ref[level]
        right = right_rows(value.astype(F32), features)
        for one in range(leaves):
            flag = far_ref[level, 0, one].astype(F32)
            weight = (value.astype(F32) * flag).astype(BF)
            add_terms(features, left_ref, sum_ref, one * leaf, leaf, right, weight)

    for level in range(levels):
        node_copy(level).wait_recv()
        if level == levels - 1:
            break
        upper = bit(level)
        pair_ref[pl.ds(pl.multiple_of(upper * SKEL, SKEL), SKEL), :] = node_ref[level].astype(F32)
        pair_ref[pl.ds(pl.multiple_of((1 - upper) * SKEL, SKEL), SKEL), :] = held_ref[level].astype(F32)
        pick_skeleton(lambda at: merge_ref[level, at], pair_ref, skel_ref, index_ref)
        node_ref[level + 1] = merged(features, pair_ref, skel_ref, index_ref)
        node_copy(level + 1).start()
        if level == 0:
            for start in range(0, count, SKEL):
                left_ref[start : start + SKEL, :] = left_rows(picked_ref[start : start + SKEL, :], features)
            sum_ref[...] = jnp.zeros_like(sum_ref)
        far_terms(level)
    last_ref[...] = held_ref[levels - 1]
    for level in range(levels):
        node_copy(level).wait_send()
    for step in range(1, slabs):
        ask_copy(step).wait_send()
        near_copy(step).wait_send()
        near_copy(step).wait_recv()


def last_kernel(features, level, slabs, far_in, target_in, node_ref, left_ref, near_ref,
                prior_ref, out_ref, sum_ref, far_ref, target_ref, input_sem):
    loads = [
        pltpu.make_async_copy(far_in, far_ref, input_sem.at[0]),
        pltpu.make_async_copy(target_in, target_ref, input_sem.at[1]),
    ]
    for load in loads:
        load.start()
    leaves = far_ref.shape[2]
    leaf = left_ref.shape[0] // leaves
    sum_ref[...] = prior_ref[...]
    value = node_ref[...]
    right = right_rows(value.astype(F32), features)
    for load in loads:
        load.wait()
    for one in range(leaves):
        @pl.when(far_ref[level, 0, one] > 0)
        def _(one=one):
            add_terms(features, left_ref, sum_ref, one * leaf, leaf, right, value)

    def one_slab(step, carry):
        owner = lax.rem(lax.axis_index("task") + step, slabs)
        for one in range(target_ref.shape[0]):
            target = target_ref[one, owner]

            @pl.when(target >= 0)
            def _():
                begin = pl.multiple_of(target * leaf, leaf)
                for start in range(0, leaf, SKEL):
                    value = near_ref[step, one * leaf + start : one * leaf + start + SKEL, :]
                    right = right_rows(value.astype(F32), features)
                    add_terms(features, left_ref, sum_ref, begin, leaf, right, value)

        return carry

    lax.fori_loop(0, slabs, one_slab, 0)
    for start in range(0, sum_ref.shape[0], SKEL):
        out_ref[:, start : start + SKEL] = sum_ref[start : start + SKEL, :].T[features:, :]


def in_hbm(value):
    return pltpu.with_memory_space_constraint(value, pltpu.HBM)


def body(points, weights, point_order, node_order, merge_order, far_list, task_target, task_source):
    count, features = points.shape
    columns = weights.shape[1]
    width = features + columns
    levels = far_list.shape[3]
    leaf = count // far_list.shape[2]
    slabs, cap = task_source.shape[2:]
    far = far_list.transpose(0, 3, 1, 2)[0]
    source = task_source[0, 0].T
    inputs = (points.T, weights.T, point_order[0, 0], node_order[0, 0], merge_order[0, 0], far, source)
    left, total, near, last = pl.pallas_call(
        functools.partial(chain_kernel, features, levels, slabs),
        out_shape=(
            jax.ShapeDtypeStruct((count, width), BF),
            jax.ShapeDtypeStruct((count, width), F32),
            jax.ShapeDtypeStruct((slabs, cap * leaf, width), BF),
            jax.ShapeDtypeStruct((SKEL, width), BF),
        ),
        in_specs=[HBM] * 7,
        out_specs=(VMEM, VMEM, VMEM, VMEM),
        scratch_shapes=[
            pltpu.VMEM((count, width), F32),
            pltpu.VMEM((count, width), F32),
            pltpu.VMEM((2 * SKEL, width), F32),
            pltpu.VMEM((SKEL, width), F32),
            pltpu.VMEM((SKEL, width), jnp.int32),
            pltpu.VMEM((levels, SKEL, width), BF),
            pltpu.VMEM((levels, SKEL, width), BF),
            pltpu.VMEM((slabs, cap, slabs), jnp.int32),
            pltpu.VMEM((slabs, cap * leaf, width), BF),
            pltpu.VMEM((features, count), BF),
            pltpu.VMEM((columns, count), BF),
            pltpu.SMEM((count,), jnp.int32),
            pltpu.SMEM((count,), jnp.int32),
            pltpu.SMEM((levels - 1, 2 * SKEL), jnp.int32),
            pltpu.SMEM(far.shape, jnp.int32),
            pltpu.VMEM(source.shape, jnp.int32),
            pltpu.SemaphoreType.DMA((7,)),
            pltpu.SemaphoreType.DMA((levels,)),
            pltpu.SemaphoreType.DMA((levels,)),
            pltpu.SemaphoreType.DMA((slabs,)),
            pltpu.SemaphoreType.DMA((slabs,)),
            pltpu.SemaphoreType.DMA((slabs,)),
            pltpu.SemaphoreType.DMA((slabs,)),
        ],
        compiler_params=pltpu.CompilerParams(
            collective_id=0, has_side_effects=True, vmem_limit_bytes=48 << 20
        ),
        name="chain",
    )(*[in_hbm(one) for one in inputs])
    target = task_target[0, 0].T
    out = pl.pallas_call(
        functools.partial(last_kernel, features, levels - 1, slabs),
        out_shape=jax.ShapeDtypeStruct((columns, count), F32),
        in_specs=[HBM, HBM, VMEM, VMEM, VMEM, VMEM],
        out_specs=VMEM,
        scratch_shapes=[
            pltpu.VMEM((count, width), F32),
            pltpu.SMEM(far.shape, jnp.int32),
            pltpu.SMEM(target.shape, jnp.int32),
            pltpu.SemaphoreType.DMA((2,)),
        ],
        compiler_params=pltpu.CompilerParams(vmem_limit_bytes=48 << 20),
        name="near_and_last",
    )(in_hbm(far), in_hbm(target), last, left, near, total)
    return out.T


def solution(mesh):
    return jax.shard_map(
        body,
        mesh=mesh,
        in_specs=(
            P(("leaf", "task"), None),
            P(("leaf", "task"), None),
            P("leaf", "task", None),
            P("leaf", "task", None),
            P("leaf", "task", None, None),
            P("leaf", "task", None, None),
            P("leaf", "task", None, None),
            P("leaf", "task", None, None),
        ),
        out_specs=P(("leaf", "task"), None),
        check_vma=False,
    )
```
